32 devices in a mesh: pair: 2 (over x), code: 2 (over core), dp: 8 (over z, y).
Axes of the slice: x: 2, y: 2, z: 4, core: 2. Of those that a mesh axis runs over, the one named last changes fastest.
Arguments:
- samples: bfloat16 [1536, 1024], P('dp'), may hold values from -48 to 48
- codebooks: bfloat16 [2, 16384, 1024], P('pair', 'code'), may hold values from -0.15625 to 0.15625
Outputs:
- new_codebooks: float32 [2, 16384, 1024], P('pair', ('code', 'dp'))
The draws below stay inside these ranges and needn't reach their ends.
All inputs are finite; a program needn't handle non-finite values.
Results may differ from the reference program's by a relative error of at most 0.015.
Values may be sent and summed in bfloat16 or wider, within the bound.
No kernel may reach another device: no remote copies, remote signals or barrier semaphores. Data moves between devices by JAX's collectives and lax.ppermute only.
A program may use at most 192 MiB of HBM per device.

```python
import jax
import jax.numpy as jnp
from jax import lax

D = 1024
K = 16384
R_DEV = 192
ROWS = 1536


def shared_books(key):
    base = jax.random.fold_in(key, 7)
    words = jax.random.truncated_normal(base, -5.0, 5.0, (2, K, D), jnp.float32) * D ** (-0.5)
    return words


def draw_codebooks(key, part):
    words = shared_books(key)
    return words.astype(jnp.bfloat16)


def draw_samples(key, part):
    values = jax.random.truncated_normal(jax.random.fold_in(key, 11), -6.0, 6.0, (ROWS, D), jnp.float32)
    return values.astype(jnp.bfloat16)


def setup_inputs(seed: int = 0) -> dict:
    seeds = jax.random.split(jax.random.key(seed), 3)
    samples = draw_samples(jax.random.fold_in(seeds[2], 71), 0)
    codebooks = draw_codebooks(jax.random.fold_in(seeds[2], 71), 0)
    return {"samples": samples, "codebooks": codebooks}


smoothing = 0.5


def logits_of(block, words, sq_norms):
    return 2.0 * jnp.dot(block, words.T, preferred_element_type=jnp.float32) - sq_norms[None, :]


def reference(samples, codebooks):
    words32 = codebooks.astype(jnp.float32)
    sq_norms = jnp.sum(words32 * words32, axis=-1)
    blocks = samples.reshape(ROWS // R_DEV, R_DEV, D)
    rebuilt_all = []
    for book in range(2):
        def rebuild(block):
            logits = logits_of(block, codebooks[book], sq_norms[book])
            top_val = jnp.max(logits, axis=1, keepdims=True)
            expd = jnp.exp(logits - top_val)
            total = jnp.sum(expd, axis=1, keepdims=True)
            summed = jnp.dot(expd.astype(jnp.bfloat16), codebooks[book], preferred_element_type=jnp.float32)
            return (summed / total).astype(jnp.bfloat16)
        rebuilt_all.append(lax.map(rebuild, blocks).reshape(ROWS, D))
    results = []
    for book in range(2):
        residual = (samples.astype(jnp.float32) - rebuilt_all[1 - book].astype(jnp.float32)).astype(jnp.bfloat16)
        res_blocks = residual.reshape(ROWS // R_DEV, R_DEV, D)

        def accumulate(carry, block):
            logits = logits_of(block, codebooks[book], sq_norms[book])
            top_val = jnp.max(logits, axis=1, keepdims=True)
            expd = jnp.exp(logits - top_val)
            total = jnp.sum(expd, axis=1, keepdims=True)
            assign = (expd / total).astype(jnp.bfloat16)
            sums = carry[0] + jnp.dot(assign.T, block, preferred_element_type=jnp.float32)
            counts = carry[1] + jnp.sum(assign.astype(jnp.float32), axis=0)
            return (sums, counts), None

        start = (jnp.zeros((K, D), jnp.float32), jnp.zeros((K,), jnp.float32))
        (sums, counts), unused = lax.scan(accumulate, start, res_blocks)
        results.append((sums + smoothing * words32[book]) / (counts[:, None] + smoothing))
    return jnp.stack(results, axis=0)
```

```python
import functools

import jax
import jax.numpy as jnp
from jax import lax
from jax.experimental import pallas as pl
from jax.experimental.pallas import tpu as pltpu
from jax.sharding import PartitionSpec as P

smoothing = 0.5
f32, bf16 = jnp.float32, jnp.bfloat16
NT = (((1,), (1,)), ((), ()))
NN = (((1,), (0,)), ((), ()))
LANES = 128


def row_norms(words):
    wide = words.astype(f32)
    return jnp.sum(wide * wide, axis=1)


def first_kernel(core, s_ref, w_ref, mine, other, sq_ref, acc, top, total, twice):
    step = pl.program_id(0)
    rows, depth = s_ref.shape

    @pl.when(step == 0)
    def _():
        acc[...] = jnp.zeros_like(acc)
        top[...] = jnp.full_like(top, -jnp.inf)
        total[...] = jnp.zeros_like(total)
        twice[...] = s_ref[...] * 2

    words = w_ref[...]
    sq = row_norms(words)[None, :]
    sq_ref[...] = sq
    logits = lax.dot_general(twice[...], words, NT, preferred_element_type=f32) - sq
    old = top[...]
    new = jnp.maximum(old, jnp.max(logits, axis=1, keepdims=True))
    expd = jnp.exp(logits - new)
    scale = jnp.exp(old - new)
    top[...] = new
    total[...] = total[...] * scale + jnp.sum(expd, axis=1, keepdims=True)
    part = lax.dot_general(expd.astype(bf16), words, NN, preferred_element_type=f32)
    acc[...] = acc[...] * scale + part

    @pl.when(step == pl.num_programs(0) - 1)
    def _():
        half = rows // 2

        def put(ref, lo):
            at = slice(lo, lo + half)
            ref[:, :depth] = acc[at]
            ref[:, depth : depth + LANES] = jnp.broadcast_to(top[at], (half, LANES))
            ref[:, depth + LANES :] = jnp.broadcast_to(total[at], (half, LANES))

        @pl.when(core[0] == 0)
        def _():
            put(mine, 0)
            put(other, half)

        @pl.when(core[0] == 1)
        def _():
            put(mine, half)
            put(other, 0)


def first_pass(core, samples, words, tile):
    rows, depth = samples.shape
    count = words.shape[0]
    half = jax.ShapeDtypeStruct((rows // 2, depth + 2 * LANES), f32)
    return pl.pallas_call(
        first_kernel,
        grid=(count // tile,),
        in_specs=[
            pl.BlockSpec(memory_space=pltpu.SMEM),
            pl.BlockSpec((rows, depth), lambda t: (0, 0)),
            pl.BlockSpec((tile, depth), lambda t: (t, 0)),
        ],
        out_specs=[pl.BlockSpec(half.shape, lambda t: (0, 0))] * 2
        + [pl.BlockSpec((1, tile), lambda t: (0, t))],
        out_shape=[half, half, jax.ShapeDtypeStruct((1, count), f32)],
        scratch_shapes=[
            pltpu.VMEM((rows, depth), f32),
            pltpu.VMEM((rows, 1), f32),
            pltpu.VMEM((rows, 1), f32),
            pltpu.VMEM((rows, depth), bf16),
        ],
        name="first_pass",
        compiler_params=pltpu.CompilerParams(vmem_limit_bytes=24 * 2**20),
    )(core, samples, words)


def stats_kernel(a_ref, b_ref, w_ref, sq_ref, lse, top, total, twice):
    step = pl.program_id(0)
    half = a_ref.shape[0]

    @pl.when(step == 0)
    def _():
        top[...] = jnp.full_like(top, -jnp.inf)
        total[...] = jnp.zeros_like(total)
        twice[:half] = a_ref[...] * 2
        twice[half:] = b_ref[...] * 2

    logits = lax.dot_general(twice[...], w_ref[...], NT, preferred_element_type=f32) - sq_ref[...]
    old = top[...]
    new = jnp.maximum(old, jnp.max(logits, axis=1, keepdims=True))
    top[...] = new
    total[...] = total[...] * jnp.exp(old - new) + jnp.sum(
        jnp.exp(logits - new), axis=1, keepdims=True
    )

    @pl.when(step == pl.num_programs(0) - 1)
    def _():
        column = top[...] + jnp.log(total[...])
        lse[...] = column.reshape(1, 2 * half)


def stats_pass(first, second, words, sq, tile):
    half, depth = first.shape
    count = words.shape[0]
    return pl.pallas_call(
        stats_kernel,
        grid=(count // tile,),
        in_specs=[
            pl.BlockSpec((half, depth), lambda t: (0, 0)),
            pl.BlockSpec((half, depth), lambda t: (0, 0)),
            pl.BlockSpec((tile, depth), lambda t: (t, 0)),
            pl.BlockSpec((1, tile), lambda t: (0, t)),
        ],
        out_specs=pl.BlockSpec((1, 2 * half), lambda t: (0, 0)),
        out_shape=jax.ShapeDtypeStruct((1, 2 * half), f32),
        scratch_shapes=[
            pltpu.VMEM((2 * half, 1), f32),
            pltpu.VMEM((2 * half, 1), f32),
            pltpu.VMEM((2 * half, depth), bf16),
        ],
        name="stats_pass",
        cost_estimate=pl.CostEstimate(
            flops=4 * half * count * depth, bytes_accessed=2 * count * depth, transcendentals=0
        ),
        compiler_params=pltpu.CompilerParams(vmem_limit_bytes=24 * 2**20),
    )(first, second, words, sq)


def last_kernel(own, w_ref, r_ref, lse_ref, out, acc, counts, sq):
    step = pl.program_id(0)

    @pl.when(step == 0)
    def _():
        acc[...] = jnp.zeros_like(acc)
        counts[...] = jnp.zeros_like(counts)
        sq[...] = row_norms(w_ref[...])[:, None]

    words = w_ref[...]
    block = r_ref[...]
    logits = 2.0 * lax.dot_general(words, block, NT, preferred_element_type=f32)
    assign = jnp.exp(logits - sq[...] - lse_ref[...]).astype(bf16)
    acc[...] += lax.dot_general(assign, block, NN, preferred_element_type=f32)
    counts[...] += jnp.sum(assign.astype(f32), axis=1, keepdims=True)

    @pl.when(step == pl.num_programs(0) - 1)
    def _():
        out[...] = (acc[...] + smoothing * words.astype(f32)) / (counts[...] + smoothing)


def last_pass(own, words, block, lse, owned, tile):
    rows, depth = block.shape
    return pl.pallas_call(
        last_kernel,
        grid_spec=pltpu.PrefetchScalarGridSpec(
            num_scalar_prefetch=1,
            grid=(rows // tile,),
            in_specs=[
                pl.BlockSpec((owned, depth), lambda t, own: (own[0], 0)),
                pl.BlockSpec((tile, depth), lambda t, own: (t, 0)),
                pl.BlockSpec((1, tile), lambda t, own: (0, t)),
            ],
            out_specs=pl.BlockSpec((owned, depth), lambda t, own: (0, 0)),
            scratch_shapes=[
                pltpu.VMEM((owned, depth), f32),
                pltpu.VMEM((owned, 1), f32),
                pltpu.VMEM((owned, 1), f32),
            ],
        ),
        out_shape=jax.ShapeDtypeStruct((owned, depth), f32),
        name="last_pass",
        compiler_params=pltpu.CompilerParams(vmem_limit_bytes=32 * 2**20),
    )(own, words, block, lse)


def to_other(value, axis, flip):
    return lax.ppermute(value, axis, [(i, i ^ flip) for i in range(lax.axis_size(axis))])


def to_column(value, step):
    n = lax.axis_size("dp")
    table = []
    for book in range(2):
        for core in range(2):
            hop = n // 2 - 1 - step if core == 0 else step
            for d in range(n):
                here = (book * 2 + core) * n + d
                there = ((1 - book) * 2 + core) * n + (d ^ (2 * hop))
                table.append((here, there))
    return lax.ppermute(value, ("pair", "code", "dp"), table)


def shards(samples, codebooks):
    words = pltpu.with_memory_space_constraint(codebooks[0], pltpu.HBM)
    rows, depth = samples.shape
    half = rows // 2
    n = lax.axis_size("dp")
    core = lax.axis_index("code")
    mine, other, sq = first_pass(core.reshape(1), samples, words, 1024)
    theirs = to_other(other, "code", 1)

    def parts(value):
        return value[:, depth : depth + 1], value[:, depth + LANES : depth + LANES + 1], value[:, :depth]

    top_a, total_a, sum_a = parts(mine)
    top_b, total_b, sum_b = parts(theirs)
    top = jnp.maximum(top_a, top_b)
    scale_a, scale_b = jnp.exp(top_a - top), jnp.exp(top_b - top)
    rebuilt = (sum_a * scale_a + sum_b * scale_b) / (total_a * scale_a + total_b * scale_b)
    own_rows = lax.dynamic_slice_in_dim(samples, core * half, half, 0)
    residual = (own_rows.astype(f32) - rebuilt.astype(bf16).astype(f32)).astype(bf16)

    direct = [to_column(residual, i) for i in range(n // 2)]
    swapped = [to_other(value, "code", 1) for value in direct]
    lse = stats_pass(direct[0], swapped[0], words, sq, 1024)
    far = to_other(lse, "code", 1)
    far = jnp.concatenate([far[:, half:], far[:, :half]], axis=1)
    lse = jnp.logaddexp(lse, far)
    flip = 1
    while flip < n:
        lse = jnp.concatenate([lse, to_other(lse, "dp", flip)], axis=0)
        flip *= 2
    near = [to_other(value, "dp", 1) for value in direct]
    near_swapped = [to_other(value, "code", 1) for value in near]
    pieces = []
    for group in zip(direct, swapped, near, near_swapped):
        pieces += group
    everything = jnp.concatenate(pieces, axis=0)
    own = lax.axis_index("dp").reshape(1)
    updated = last_pass(
        own, words, everything, lse.reshape(1, n * rows), words.shape[0] // n, 2 * rows
    )
    return updated[None]


def solution(mesh):
    in_specs = (P("dp", None), P("pair", "code", None))
    out_specs = P("pair", ("code", "dp"), None)
    return jax.shard_map(shards, mesh=mesh, in_specs=in_specs, out_specs=out_specs, check_vma=False)
```

```python
import functools

import jax
import jax.numpy as jnp
from jax import lax
from jax.experimental import pallas as pl
from jax.experimental.pallas import tpu as pltpu
from jax.sharding import PartitionSpec as P


smoothing = 0.5
f32, bf16 = jnp.float32, jnp.bfloat16
NT = (((1,), (1,)), ((), ()))
NN = (((1,), (0,)), ((), ()))
TN = (((0,), (0,)), ((), ()))
LANES = 128
SUBLANES = 8
AHEAD = 2
VMEM = pl.BlockSpec(memory_space=pltpu.VMEM)
SMEM = pl.BlockSpec(memory_space=pltpu.SMEM)
HBM = pl.BlockSpec(memory_space=pltpu.HBM)


def square_sums(words):
    wide = words.astype(f32)
    return jnp.sum(wide * wide, axis=1, keepdims=True)


def span(t, tile):
    return pl.ds(pl.multiple_of(t * tile, tile), tile)


def tile_copy(source, held, sems, tile, t):
    at = span(t, tile)
    return pltpu.make_async_copy(source.at[at], held.at[at], sems.at[t])


def first_kernel(tile, core, s_hbm, w_hbm, mine, other, held, acc, top, twice, logits, sems, own_sem):
    rows, depth = twice.shape
    steps = w_hbm.shape[0] // tile
    fetch = pltpu.make_async_copy(s_hbm, twice, own_sem.at[0])
    fetch.start()
    for t in range(min(AHEAD, steps)):
        tile_copy(w_hbm, held, sems, tile, t).start()
    fetch.wait()
    twice[...] = twice[...] * 2
    top[...] = jnp.full_like(top, -jnp.inf)

    @pl.loop(0, steps)
    def _(t):
        @pl.when(t + AHEAD < steps)
        def _():
            tile_copy(w_hbm, held, sems, tile, t + AHEAD).start()

        tile_copy(w_hbm, held, sems, tile, t).wait()
        words = held[span(t, tile)]
        score = lax.dot_general(words, twice[...], NT, preferred_element_type=f32)
        score = score - square_sums(words)
        logits[span(t, tile)] = score
        groups = score.reshape(tile // SUBLANES, SUBLANES, rows)
        top[...] = jnp.maximum(top[...], jnp.max(groups, axis=0))

    best = jnp.max(top[...], axis=0, keepdims=True)
    acc[...] = jnp.zeros_like(acc)

    def add(t, total):
        expd = jnp.exp(logits[span(t, tile)] - best)
        acc[...] += lax.dot_general(
            expd.astype(bf16), held[span(t, tile)], TN, preferred_element_type=f32
        )
        return total + jnp.sum(expd.reshape(tile // SUBLANES, SUBLANES, rows), axis=0)

    total = lax.fori_loop(0, steps, add, jnp.zeros((SUBLANES, rows), f32))
    total = jnp.sum(total, axis=0, keepdims=True)
    tops = jnp.broadcast_to(best.reshape(rows, 1), (rows, LANES))
    totals = jnp.broadcast_to(total.reshape(rows, 1), (rows, LANES))
    half = rows // 2

    def put(ref, lo):
        at = slice(lo, lo + half)
        ref[:, :depth] = acc[at]
        ref[:, depth : depth + LANES] = tops[at]
        ref[:, depth + LANES :] = totals[at]

    @pl.when(core[0] == 0)
    def _():
        put(mine, 0)
        put(other, half)

    @pl.when(core[0] == 1)
    def _():
        put(mine, half)
        put(other, 0)


def first_pass(core, samples, words, tile):
    rows, depth = samples.shape
    count = words.shape[0]
    half = jax.ShapeDtypeStruct((rows // 2, depth + 2 * LANES), f32)
    return pl.pallas_call(
        functools.partial(first_kernel, tile),
        in_specs=[SMEM, HBM, HBM],
        out_specs=[VMEM, VMEM],
        out_shape=[half, half],
        scratch_shapes=[
            pltpu.VMEM((count, depth), bf16),
            pltpu.VMEM((rows, depth), f32),
            pltpu.VMEM((SUBLANES, rows), f32),
            pltpu.VMEM((rows, depth), bf16),
            pltpu.VMEM((count, rows), f32),
            pltpu.SemaphoreType.DMA((count // tile,)),
            pltpu.SemaphoreType.DMA((1,)),
        ],
        name="first_pass",
        compiler_params=pltpu.CompilerParams(vmem_limit_bytes=40 * 2**20),
    )(core, samples, words)


def join(core, samples, mine, theirs):
    half, depth = samples.shape[0] // 2, samples.shape[1]

    def parts(value):
        return value[:, depth : depth + 1], value[:, depth + LANES : depth + LANES + 1], value[:, :depth]

    top_a, total_a, sum_a = parts(mine)
    top_b, total_b, sum_b = parts(theirs)
    top = jnp.maximum(top_a, top_b)
    scale_a, scale_b = jnp.exp(top_a - top), jnp.exp(top_b - top)
    rebuilt = (sum_a * scale_a + sum_b * scale_b) / (total_a * scale_a + total_b * scale_b)
    own = lax.dynamic_slice_in_dim(samples, core[0] * half, half, 0)
    return (own.astype(f32) - rebuilt.astype(bf16).astype(f32)).astype(bf16)


def stats_kernel(tile, a_hbm, b_hbm, w_hbm, lse, held, top, total, twice, sems, row_sems):
    half = a_hbm.shape[0]
    steps = held.shape[0] // tile
    fetches = [
        pltpu.make_async_copy(source, twice.at[pl.ds(i * half, half)], row_sems.at[i])
        for i, source in enumerate((a_hbm, b_hbm))
    ]
    for fetch in fetches:
        fetch.start()
    for t in range(min(AHEAD, steps)):
        tile_copy(w_hbm, held, sems, tile, t).start()
    for fetch in fetches:
        fetch.wait()
    twice[...] = twice[...] * 2
    top[...] = jnp.full_like(top, -jnp.inf)
    total[...] = jnp.zeros_like(total)

    @pl.loop(0, steps)
    def _(t):
        @pl.when(t + AHEAD < steps)
        def _():
            tile_copy(w_hbm, held, sems, tile, t + AHEAD).start()

        tile_copy(w_hbm, held, sems, tile, t).wait()
        words = held[span(t, tile)]
        score = lax.dot_general(words, twice[...], NT, preferred_element_type=f32)
        score = (score - square_sums(words)).reshape(tile // SUBLANES, SUBLANES, 2 * half)
        old = top[...]
        new = jnp.maximum(old, jnp.max(score, axis=0))
        total[...] = total[...] * jnp.exp(old - new) + jnp.sum(jnp.exp(score - new[None]), axis=0)
        top[...] = new

    best = jnp.max(top[...], axis=0, keepdims=True)
    lse[...] = best + jnp.log(jnp.sum(total[...] * jnp.exp(top[...] - best), axis=0, keepdims=True))


def stats_pass(first, second, words, tile):
    half, depth = first.shape
    count = words.shape[0]
    return pl.pallas_call(
        functools.partial(stats_kernel, tile),
        in_specs=[HBM, HBM, HBM],
        out_specs=VMEM,
        out_shape=jax.ShapeDtypeStruct((1, 2 * half), f32),
        scratch_shapes=[
            pltpu.VMEM((count, depth), bf16),
            pltpu.VMEM((SUBLANES, 2 * half), f32),
            pltpu.VMEM((SUBLANES, 2 * half), f32),
            pltpu.VMEM((2 * half, depth), bf16),
            pltpu.SemaphoreType.DMA((count // tile,)),
            pltpu.SemaphoreType.DMA((2,)),
        ],
        name="stats_pass",
        cost_estimate=pl.CostEstimate(
            flops=4 * half * count * depth, bytes_accessed=2 * count * depth, transcendentals=0
        ),
        compiler_params=pltpu.CompilerParams(vmem_limit_bytes=60 * 2**20),
    )(first, second, words)


def row_fetches(pieces, block, sems, first):
    fetches, at = [], 0
    for i, piece in enumerate(pieces):
        rows = piece.shape[0]
        fetches.append(pltpu.make_async_copy(piece, block.at[pl.ds(at, rows)], sems.at[first + i]))
        at += rows
    return fetches


def score_kernel(count, own, w_hbm, *refs):
    pieces, (logits, block, words, sems) = refs[:count], refs[count:]
    fetch = pltpu.make_async_copy(w_hbm.at[span(own[0], words.shape[0])], words, sems.at[count])
    fetch.start()
    fetches = row_fetches(pieces, block, sems, 0)
    for other in fetches:
        other.start()
    fetch.wait()
    sq = square_sums(words[...])
    for other in fetches:
        other.wait()
    score = lax.dot_general(words[...] * 2, block[...], NT, preferred_element_type=f32)
    logits[...] = score - sq


def score_pass(own, words, pieces, owned):
    depth = words.shape[1]
    rows = sum(piece.shape[0] for piece in pieces)
    return pl.pallas_call(
        functools.partial(score_kernel, len(pieces)),
        in_specs=[SMEM, HBM] + [HBM] * len(pieces),
        out_specs=VMEM,
        scratch_shapes=[
            pltpu.VMEM((rows, depth), bf16),
            pltpu.VMEM((owned, depth), bf16),
            pltpu.SemaphoreType.DMA((len(pieces) + 1,)),
        ],
        out_shape=jax.ShapeDtypeStruct((owned, rows), f32),
        name="score_pass",
        cost_estimate=pl.CostEstimate(
            flops=2 * owned * rows * depth, bytes_accessed=2 * rows * depth, transcendentals=0
        ),
        compiler_params=pltpu.CompilerParams(vmem_limit_bytes=40 * 2**20),
    )(own, words, *pieces)


def last_kernel(count, tile, chunk, own, w_hbm, la_ref, lse_ref, *refs):
    near, direct = refs[:count], refs[count : 2 * count]
    out, block, words, assign, staged, sems, out_sems = refs[2 * count :]
    owned = words.shape[0]
    rows = la_ref.shape[1]
    fetch = pltpu.make_async_copy(w_hbm.at[span(own[0], owned)], words, sems.at[2 * count])
    fetch.start()
    fetches = row_fetches(near, block.at[pl.ds(rows, rows)], sems, 0)
    fetches += row_fetches(direct, block.at[pl.ds(0, rows)], sems, count)
    for other in fetches:
        other.start()
    assign[:, :rows] = jnp.exp(la_ref[...] - lse_ref[0:1]).astype(bf16)
    fetch.wait()
    sq = square_sums(words[...])
    twice = words[...] * 2
    each = near[0].shape[0]
    for lo in range(0, rows, chunk):
        for other in fetches[lo // each : (lo + chunk) // each]:
            other.wait()
        at = slice(rows + lo, rows + lo + chunk)
        score = lax.dot_general(twice, block[at], NT, preferred_element_type=f32)
        assign[:, at] = jnp.exp(score - sq - lse_ref[1:2, lo : lo + chunk]).astype(bf16)
    for other in fetches[count:]:
        other.wait()
    sends = []
    for lo in range(0, owned, tile):
        at = slice(lo, lo + tile)
        sums = lax.dot_general(assign[at], block[...], NN, preferred_element_type=f32)
        counts = jnp.sum(assign[at].astype(f32), axis=1, keepdims=True)
        staged[at] = (sums + smoothing * words[at].astype(f32)) / (counts + smoothing)
        sends.append(pltpu.make_async_copy(staged.at[at], out.at[at], out_sems.at[lo // tile]))
        sends[-1].start()
    for send in sends:
        send.wait()


def last_pass(own, words, scored, lse, near, direct, owned, tile, chunk):
    depth = words.shape[1]
    rows = scored.shape[1]
    count = len(near)
    return pl.pallas_call(
        functools.partial(last_kernel, count, tile, chunk),
        in_specs=[SMEM, HBM, VMEM, VMEM] + [HBM] * (2 * count),
        out_specs=HBM,
        scratch_shapes=[
            pltpu.VMEM((2 * rows, depth), bf16),
            pltpu.VMEM((owned, depth), bf16),
            pltpu.VMEM((owned, 2 * rows), bf16),
            pltpu.VMEM((owned, depth), f32),
            pltpu.SemaphoreType.DMA((2 * count + 1,)),
            pltpu.SemaphoreType.DMA((owned // tile,)),
        ],
        out_shape=jax.ShapeDtypeStruct((owned, depth), f32),
        name="last_pass",
        compiler_params=pltpu.CompilerParams(vmem_limit_bytes=50 * 2**20),
    )(own, words, scored, lse, *near, *direct)


def to_other(value, axis, flip):
    return lax.ppermute(value, axis, [(i, i ^ flip) for i in range(lax.axis_size(axis))])


def to_column(value, step):
    n = lax.axis_size("dp")
    table = []
    for book in range(2):
        for core in range(2):
            hop = step ^ 1 if core == 0 else step ^ 1 ^ (n // 2 - 1)
            for d in range(n):
                here = (book * 2 + core) * n + d
                there = ((1 - book) * 2 + core) * n + (d ^ (2 * hop))
                table.append((here, there))
    return lax.ppermute(value, ("pair", "code", "dp"), table)


def hbm_named(call, *args):
    return pltpu.with_memory_space_constraint(call(*args), pltpu.HBM)


def step(samples, codebooks):
    words = pltpu.with_memory_space_constraint(codebooks[0], pltpu.HBM)
    rows, _ = samples.shape
    half = rows // 2
    n = lax.axis_size("dp")
    owned = words.shape[0] // n
    core = lax.axis_index("code").reshape(1)
    own = lax.axis_index("dp").reshape(1)
    mine, other = first_pass(
        core, pltpu.with_memory_space_constraint(samples, pltpu.HBM), words, 1024
    )
    theirs = to_other(other, "code", 1)
    residual = join(core, samples, mine, theirs)

    direct = [hbm_named(to_column, residual, i) for i in range(n // 2)]
    swapped = [hbm_named(to_other, direct[i], "code", 1) for i in range(n // 2)]
    near = [hbm_named(to_other, direct[i], "dp", 1) for i in range(n // 2)]
    near_swapped = [hbm_named(to_other, near[i], "code", 1) for i in range(n // 2)]

    lse = stats_pass(direct[0], swapped[0], words, 1024)
    far = to_other(lse, "code", 1)
    far = jnp.concatenate([far[:, half:], far[:, :half]], axis=1)
    lse = jnp.logaddexp(lse, far)
    flip = 1
    while flip < n:
        lse = jnp.concatenate([lse, to_other(lse, "dp", flip)], axis=0)
        flip *= 2
    lse = jnp.stack([lse[0::2].reshape(-1), lse[1::2].reshape(-1)])

    direct = [v for pair in zip(direct, swapped) for v in pair]
    near = [v for pair in zip(near, near_swapped) for v in pair]
    scored = score_pass(own, words, direct, owned)
    updated = last_pass(
        own, words, scored, lse, near, direct, owned, max(owned // 4, 128), 2 * rows
    )
    return updated[None]


def solution(mesh):
    in_specs = (P("dp", None), P("pair", "code", None))
    out_specs = P("pair", ("code", "dp"), None)
    return jax.shard_map(step, mesh=mesh, in_specs=in_specs, out_specs=out_specs, check_vma=False)
```

```python
import functools

import jax
import jax.numpy as jnp
from jax import lax
from jax.experimental import pallas as pl
from jax.experimental.pallas import tpu as pltpu
from jax.sharding import PartitionSpec as P


smoothing = 0.5
f32, bf16 = jnp.float32, jnp.bfloat16
NT = (((1,), (1,)), ((), ()))
NN = (((1,), (0,)), ((), ()))
TN = (((0,), (0,)), ((), ()))
LANES = 128
SUBLANES = 8
AHEAD = 2
VMEM = pl.BlockSpec(memory_space=pltpu.VMEM)
SMEM = pl.BlockSpec(memory_space=pltpu.SMEM)
HBM = pl.BlockSpec(memory_space=pltpu.HBM)
ANY = pl.BlockSpec(memory_space=pl.ANY)


def square_sums(words):
    wide = words.astype(f32)
    return jnp.sum(wide * wide, axis=1, keepdims=True)


def span(t, tile):
    return pl.ds(pl.multiple_of(t * tile, tile), tile)


def tile_copy(source, held, sems, tile, t):
    at = span(t, tile)
    return pltpu.make_async_copy(source.at[at], held.at[at], sems.at[t])


def first_kernel(tile, core, s_hbm, w_hbm, mine, other, held, acc, top, twice, logits, sems, own_sem):
    rows, depth = twice.shape
    steps = w_hbm.shape[0] // tile
    fetch = pltpu.make_async_copy(s_hbm, twice, own_sem.at[0])
    fetch.start()
    for t in range(min(AHEAD, steps)):
        tile_copy(w_hbm, held, sems, tile, t).start()
    fetch.wait()
    twice[...] = twice[...] * 2
    top[...] = jnp.full_like(top, -jnp.inf)

    @pl.loop(0, steps)
    def _(t):
        @pl.when(t + AHEAD < steps)
        def _():
            tile_copy(w_hbm, held, sems, tile, t + AHEAD).start()

        tile_copy(w_hbm, held, sems, tile, t).wait()
        words = held[span(t, tile)]
        score = lax.dot_general(words, twice[...], NT, preferred_element_type=f32)
        score = score - square_sums(words)
        logits[span(t, tile)] = score
        groups = score.reshape(tile // SUBLANES, SUBLANES, rows)
        top[...] = jnp.maximum(top[...], jnp.max(groups, axis=0))

    best = jnp.max(top[...], axis=0, keepdims=True)
    acc[...] = jnp.zeros_like(acc)

    def add(t, total):
        expd = jnp.exp(logits[span(t, tile)] - best)
        acc[...] += lax.dot_general(
            expd.astype(bf16), held[span(t, tile)], TN, preferred_element_type=f32
        )
        return total + jnp.sum(expd.reshape(tile // SUBLANES, SUBLANES, rows), axis=0)

    total = lax.fori_loop(0, steps, add, jnp.zeros((SUBLANES, rows), f32))
    total = jnp.sum(total, axis=0, keepdims=True)
    tops = jnp.broadcast_to(best.reshape(rows, 1), (rows, LANES))
    totals = jnp.broadcast_to(total.reshape(rows, 1), (rows, LANES))
    half = rows // 2

    def put(ref, lo):
        at = slice(lo, lo + half)
        ref[:, :depth] = acc[at]
        ref[:, depth : depth + LANES] = tops[at]
        ref[:, depth + LANES :] = totals[at]

    @pl.when(core[0] == 0)
    def _():
        put(mine, 0)
        put(other, half)

    @pl.when(core[0] == 1)
    def _():
        put(mine, half)
        put(other, 0)


def first_pass(core, samples, words, tile):
    rows, depth = samples.shape
    count = words.shape[0]
    half = jax.ShapeDtypeStruct((rows // 2, depth + 2 * LANES), f32)
    return pl.pallas_call(
        functools.partial(first_kernel, tile),
        in_specs=[SMEM, HBM, HBM],
        out_specs=[VMEM, VMEM],
        out_shape=[half, half],
        scratch_shapes=[
            pltpu.VMEM((count, depth), bf16),
            pltpu.VMEM((rows, depth), f32),
            pltpu.VMEM((SUBLANES, rows), f32),
            pltpu.VMEM((rows, depth), bf16),
            pltpu.VMEM((count, rows), f32),
            pltpu.SemaphoreType.DMA((count // tile,)),
            pltpu.SemaphoreType.DMA((1,)),
        ],
        name="first_pass",
        compiler_params=pltpu.CompilerParams(vmem_limit_bytes=40 * 2**20),
    )(core, samples, words)


def join(core, samples, mine, theirs):
    half, depth = samples.shape[0] // 2, samples.shape[1]

    def parts(value):
        return value[:, depth : depth + 1], value[:, depth + LANES : depth + LANES + 1], value[:, :depth]

    top_a, total_a, sum_a = parts(mine)
    top_b, total_b, sum_b = parts(theirs)
    top = jnp.maximum(top_a, top_b)
    scale_a, scale_b = jnp.exp(top_a - top), jnp.exp(top_b - top)
    rebuilt = (sum_a * scale_a + sum_b * scale_b) / (total_a * scale_a + total_b * scale_b)
    own = lax.dynamic_slice_in_dim(samples, core[0] * half, half, 0)
    return (own.astype(f32) - rebuilt.astype(bf16).astype(f32)).astype(bf16)


def early_kernel(held, out):
    out[...] = held[: out.shape[0], : out.shape[1]]


def early_pass(words):
    return pl.pallas_call(
        early_kernel,
        in_specs=[VMEM],
        out_specs=VMEM,
        out_shape=jax.ShapeDtypeStruct((2 * SUBLANES, LANES), words.dtype),
        name="early_pass",
        compiler_params=pltpu.CompilerParams(vmem_limit_bytes=2**20),
    )(words)


def stats_kernel(tile, core, a_hbm, b_hbm, held, early, lse, top, total, twice, row_sems):
    half = a_hbm.shape[0]
    steps = held.shape[0] // tile
    fetches = [
        pltpu.make_async_copy(source, twice.at[span(place, half)], row_sems.at[i])
        for i, (source, place) in enumerate(((a_hbm, core[0]), (b_hbm, 1 - core[0])))
    ]
    for fetch in fetches:
        fetch.start()
    for fetch in fetches:
        fetch.wait()
    twice[...] = twice[...] * 2
    top[...] = jnp.full_like(top, -jnp.inf)
    total[...] = jnp.zeros_like(total)

    @pl.loop(0, steps)
    def _(t):
        words = held[span(t, tile)]
        score = lax.dot_general(words, twice[...], NT, preferred_element_type=f32)
        score = (score - square_sums(words)).reshape(tile // SUBLANES, SUBLANES, 2 * half)
        old = top[...]
        new = jnp.maximum(old, jnp.max(score, axis=0))
        total[...] = total[...] * jnp.exp(old - new) + jnp.sum(jnp.exp(score - new[None]), axis=0)
        top[...] = new

    best = jnp.max(top[...], axis=0, keepdims=True)
    lse[...] = best + jnp.log(jnp.sum(total[...] * jnp.exp(top[...] - best), axis=0, keepdims=True))


def stats_pass(core, first, second, words, early, tile):
    half, depth = first.shape
    count = words.shape[0]
    return pl.pallas_call(
        functools.partial(stats_kernel, tile),
        in_specs=[SMEM, ANY, ANY, VMEM, ANY],
        out_specs=VMEM,
        out_shape=jax.ShapeDtypeStruct((1, 2 * half), f32),
        scratch_shapes=[
            pltpu.VMEM((SUBLANES, 2 * half), f32),
            pltpu.VMEM((SUBLANES, 2 * half), f32),
            pltpu.VMEM((2 * half, depth), bf16),
            pltpu.SemaphoreType.DMA((2,)),
        ],
        name="stats_pass",
        cost_estimate=pl.CostEstimate(
            flops=4 * half * count * depth, bytes_accessed=2 * count * depth, transcendentals=0
        ),
        compiler_params=pltpu.CompilerParams(vmem_limit_bytes=24 * 2**20),
    )(core, first, second, words, early)


def row_fetches(core, pieces, block, sems, first):
    fetches = []
    for i, piece in enumerate(pieces):
        half = piece.shape[0]
        place = i - i % 2 + (core[0] if i % 2 == 0 else 1 - core[0])
        fetches.append(pltpu.make_async_copy(piece, block.at[span(place, half)], sems.at[first + i]))
    return fetches


def score_kernel(count, core, own, w_hbm, *refs):
    pieces, (logits, block, words, sems) = refs[:count], refs[count:]
    fetch = pltpu.make_async_copy(w_hbm.at[span(own[0], words.shape[0])], words, sems.at[count])
    fetch.start()
    fetches = row_fetches(core, pieces, block, sems, 0)
    for other in fetches:
        other.start()
    fetch.wait()
    sq = square_sums(words[...])
    for other in fetches:
        other.wait()
    score = lax.dot_general(words[...] * 2, block[...], NT, preferred_element_type=f32)
    logits[...] = score - sq


def score_pass(core, own, words, pieces, owned):
    depth = words.shape[1]
    rows = sum(piece.shape[0] for piece in pieces)
    return pl.pallas_call(
        functools.partial(score_kernel, len(pieces)),
        in_specs=[SMEM, SMEM, HBM] + [HBM] * len(pieces),
        out_specs=VMEM,
        scratch_shapes=[
            pltpu.VMEM((rows, depth), bf16),
            pltpu.VMEM((owned, depth), bf16),
            pltpu.SemaphoreType.DMA((len(pieces) + 1,)),
        ],
        out_shape=jax.ShapeDtypeStruct((owned, rows), f32),
        name="score_pass",
        cost_estimate=pl.CostEstimate(
            flops=2 * owned * rows * depth, bytes_accessed=2 * rows * depth, transcendentals=0
        ),
        compiler_params=pltpu.CompilerParams(vmem_limit_bytes=40 * 2**20),
    )(core, own, words, *pieces)


def last_kernel(count, tile, chunk, core, own, w_hbm, la_ref, lse_ref, *refs):
    near, direct = refs[:count], refs[count : 2 * count]
    out, block, words, assign, staged, sems, out_sems = refs[2 * count :]
    owned = words.shape[0]
    rows = la_ref.shape[1]
    fetch = pltpu.make_async_copy(w_hbm.at[span(own[0], owned)], words, sems.at[2 * count])
    fetch.start()
    fetches = row_fetches(core, near, block.at[pl.ds(rows, rows)], sems, 0)
    fetches += row_fetches(core, direct, block.at[pl.ds(0, rows)], sems, count)
    for other in fetches:
        other.start()
    assign[:, :rows] = jnp.exp(la_ref[...] - lse_ref[0:1]).astype(bf16)
    fetch.wait()
    sq = square_sums(words[...])
    twice = words[...] * 2
    each = near[0].shape[0]
    for lo in range(0, rows, chunk):
        for other in fetches[lo // each : (lo + chunk) // each]:
            other.wait()
        at = slice(rows + lo, rows + lo + chunk)
        score = lax.dot_general(twice, block[at], NT, preferred_element_type=f32)
        assign[:, at] = jnp.exp(score - sq - lse_ref[1:2, lo : lo + chunk]).astype(bf16)
    for other in fetches[count:]:
        other.wait()
    sends = []
    for lo in range(0, owned, tile):
        at = slice(lo, lo + tile)
        sums = lax.dot_general(assign[at], block[...], NN, preferred_element_type=f32)
        counts = jnp.sum(assign[at].astype(f32), axis=1, keepdims=True)
        staged[at] = (sums + smoothing * words[at].astype(f32)) / (counts + smoothing)
        sends.append(pltpu.make_async_copy(staged.at[at], out.at[at], out_sems.at[lo // tile]))
        sends[-1].start()
    for send in sends:
        send.wait()


def last_pass(core, own, words, scored, lse, near, direct, owned, tile, chunk):
    depth = words.shape[1]
    rows = scored.shape[1]
    count = len(near)
    return pl.pallas_call(
        functools.partial(last_kernel, count, tile, chunk),
        in_specs=[SMEM, SMEM, HBM, VMEM, VMEM] + [HBM] * (2 * count),
        out_specs=HBM,
        scratch_shapes=[
            pltpu.VMEM((2 * rows, depth), bf16),
            pltpu.VMEM((owned, depth), bf16),
            pltpu.VMEM((owned, 2 * rows), bf16),
            pltpu.VMEM((owned, depth), f32),
            pltpu.SemaphoreType.DMA((2 * count + 1,)),
            pltpu.SemaphoreType.DMA((owned // tile,)),
        ],
        out_shape=jax.ShapeDtypeStruct((owned, depth), f32),
        name="last_pass",
        compiler_params=pltpu.CompilerParams(vmem_limit_bytes=50 * 2**20),
    )(core, own, words, scored, lse, *near, *direct)


def to_other(value, axis, flip):
    return lax.ppermute(value, axis, [(i, i ^ flip) for i in range(lax.axis_size(axis))])


def to_column(value, step):
    n = lax.axis_size("dp")
    table = []
    for book in range(2):
        for core in range(2):
            for d in range(n):
                here = (book * 2 + core) * n + d
                there = ((1 - book) * 2 + core) * n + (d ^ (2 * step))
                table.append((here, there))
    return lax.ppermute(value, ("pair", "code", "dp"), table)


def in_hbm(value):
    return pltpu.with_memory_space_constraint(value, pltpu.HBM)


def step(samples, codebooks):
    words = pltpu.with_memory_space_constraint(codebooks[0], pltpu.HBM)
    resident = pltpu.with_memory_space_constraint(codebooks[0], pltpu.VMEM)
    rows, _ = samples.shape
    n = lax.axis_size("dp")
    owned = words.shape[0] // n
    core = lax.axis_index("code").reshape(1)
    own = lax.axis_index("dp").reshape(1)
    mine, other = first_pass(
        core, pltpu.with_memory_space_constraint(samples, pltpu.HBM), words, 1024
    )
    theirs = to_other(other, "code", 1)
    residual = join(core, samples, mine, theirs)

    direct = [to_column(residual, i) for i in range(n // 2)]
    swapped = [to_other(direct[i], "code", 1) for i in range(n // 2)]
    near = [to_other(direct[i], "dp", 1) for i in range(n // 2)]
    near_swapped = [to_other(near[i], "code", 1) for i in range(n // 2)]

    early = early_pass(resident)
    lse = stats_pass(core, direct[0], swapped[0], resident, early, 1024)
    lse = jnp.logaddexp(lse, to_other(lse, "code", 1))
    flip = 1
    while flip < n:
        lse = jnp.concatenate([lse, to_other(lse, "dp", flip)], axis=0)
        flip *= 2
    lse = jnp.stack([lse[0::2].reshape(-1), lse[1::2].reshape(-1)])

    direct = [in_hbm(v) for pair in zip(direct, swapped) for v in pair]
    near = [in_hbm(v) for pair in zip(near, near_swapped) for v in pair]
    scored = score_pass(core, own, words, direct, owned)
    updated = last_pass(
        *(core, own, words, scored, lse, near, direct, owned, max(owned // 4, 128), 2 * rows),
    )
    return updated[None]


def solution(mesh):
    in_specs = (P("dp", None), P("pair", "code", None))
    out_specs = P("pair", ("code", "dp"), None)
    return jax.shard_map(step, mesh=mesh, in_specs=in_specs, out_specs=out_specs, check_vma=False)
```

```python
import functools

import jax
import jax.numpy as jnp
from jax import lax
from jax.experimental import pallas as pl
from jax.experimental.pallas import tpu as pltpu
from jax.sharding import PartitionSpec as P


smoothing = 0.5
f32, bf16 = jnp.float32, jnp.bfloat16
NT = (((1,), (1,)), ((), ()))
NN = (((1,), (0,)), ((), ()))
TN = (((0,), (0,)), ((), ()))
LANES = 128
SUBLANES = 8
AHEAD = 2
VMEM = pl.BlockSpec(memory_space=pltpu.VMEM)
SMEM = pl.BlockSpec(memory_space=pltpu.SMEM)
HBM = pl.BlockSpec(memory_space=pltpu.HBM)
ANY = pl.BlockSpec(memory_space=pl.ANY)


def square_sums(words):
    wide = words.astype(f32)
    return jnp.sum(wide * wide, axis=1, keepdims=True)


def span(t, tile):
    return pl.ds(pl.multiple_of(t * tile, tile), tile)


def tile_copy(source, held, sems, tile, t):
    at = span(t, tile)
    return pltpu.make_async_copy(source.at[at], held.at[at], sems.at[t])


def first_kernel(tile, core, s_hbm, w_hbm, mine, other, held, acc, top, twice, logits, sems, own_sem):
    rows, depth = twice.shape
    steps = w_hbm.shape[0] // tile
    fetch = pltpu.make_async_copy(s_hbm, twice, own_sem.at[0])
    fetch.start()
    for t in range(min(AHEAD, steps)):
        tile_copy(w_hbm, held, sems, tile, t).start()
    fetch.wait()
    twice[...] = twice[...] * 2
    top[...] = jnp.full_like(top, -jnp.inf)

    @pl.loop(0, steps)
    def _(t):
        @pl.when(t + AHEAD < steps)
        def _():
            tile_copy(w_hbm, held, sems, tile, t + AHEAD).start()

        tile_copy(w_hbm, held, sems, tile, t).wait()
        words = held[span(t, tile)]
        score = lax.dot_general(words, twice[...], NT, preferred_element_type=f32)
        score = score - square_sums(words)
        logits[span(t, tile)] = score
        groups = score.reshape(tile // SUBLANES, SUBLANES, rows)
        top[...] = jnp.maximum(top[...], jnp.max(groups, axis=0))

    best = jnp.max(top[...], axis=0, keepdims=True)
    acc[...] = jnp.zeros_like(acc)

    def add(t, total):
        expd = jnp.exp(logits[span(t, tile)] - best)
        acc[...] += lax.dot_general(
            expd.astype(bf16), held[span(t, tile)], TN, preferred_element_type=f32
        )
        return total + jnp.sum(expd.reshape(tile // SUBLANES, SUBLANES, rows), axis=0)

    total = lax.fori_loop(0, steps, add, jnp.zeros((SUBLANES, rows), f32))
    total = jnp.sum(total, axis=0, keepdims=True)
    tops = jnp.broadcast_to(best.reshape(rows, 1), (rows, LANES))
    totals = jnp.broadcast_to(total.reshape(rows, 1), (rows, LANES))
    half = rows // 2

    def put(ref, lo):
        at = slice(lo, lo + half)
        ref[:, :depth] = acc[at]
        ref[:, depth : depth + LANES] = tops[at]
        ref[:, depth + LANES :] = totals[at]

    @pl.when(core[0] == 0)
    def _():
        put(mine, 0)
        put(other, half)

    @pl.when(core[0] == 1)
    def _():
        put(mine, half)
        put(other, 0)


def first_pass(core, samples, words, tile):
    rows, depth = samples.shape
    count = words.shape[0]
    half = jax.ShapeDtypeStruct((rows // 2, depth + 2 * LANES), f32)
    return pl.pallas_call(
        functools.partial(first_kernel, tile),
        in_specs=[SMEM, HBM, HBM],
        out_specs=[VMEM, VMEM],
        out_shape=[half, half],
        scratch_shapes=[
            pltpu.VMEM((count, depth), bf16),
            pltpu.VMEM((rows, depth), f32),
            pltpu.VMEM((SUBLANES, rows), f32),
            pltpu.VMEM((rows, depth), bf16),
            pltpu.VMEM((count, rows), f32),
            pltpu.SemaphoreType.DMA((count // tile,)),
            pltpu.SemaphoreType.DMA((1,)),
        ],
        name="first_pass",
        compiler_params=pltpu.CompilerParams(vmem_limit_bytes=40 * 2**20),
    )(core, samples, words)


def join(core, samples, mine, theirs):
    half, depth = samples.shape[0] // 2, samples.shape[1]

    def parts(value):
        return value[:, depth : depth + 1], value[:, depth + LANES : depth + LANES + 1], value[:, :depth]

    top_a, total_a, sum_a = parts(mine)
    top_b, total_b, sum_b = parts(theirs)
    top = jnp.maximum(top_a, top_b)
    scale_a, scale_b = jnp.exp(top_a - top), jnp.exp(top_b - top)
    rebuilt = (sum_a * scale_a + sum_b * scale_b) / (total_a * scale_a + total_b * scale_b)
    own = lax.dynamic_slice_in_dim(samples, core[0] * half, half, 0)
    return (own.astype(f32) - rebuilt.astype(bf16).astype(f32)).astype(bf16)


def early_kernel(held, out):
    out[...] = held[: out.shape[0], : out.shape[1]]


def early_pass(words):
    return pl.pallas_call(
        early_kernel,
        in_specs=[VMEM],
        out_specs=VMEM,
        out_shape=jax.ShapeDtypeStruct((2 * SUBLANES, LANES), words.dtype),
        name="early_pass",
        compiler_params=pltpu.CompilerParams(vmem_limit_bytes=2**20),
    )(words)


def stats_kernel(tile, core, a_hbm, b_hbm, held, early, lse, top, total, twice, row_sems):
    half = a_hbm.shape[0]
    steps = held.shape[0] // tile
    fetches = [
        pltpu.make_async_copy(source, twice.at[span(place, half)], row_sems.at[i])
        for i, (source, place) in enumerate(((a_hbm, core[0]), (b_hbm, 1 - core[0])))
    ]
    for fetch in fetches:
        fetch.start()
    for fetch in fetches:
        fetch.wait()
    twice[...] = twice[...] * 2
    top[...] = jnp.full_like(top, -jnp.inf)
    total[...] = jnp.zeros_like(total)

    @pl.loop(0, steps)
    def _(t):
        words = held[span(t, tile)]
        score = lax.dot_general(words, twice[...], NT, preferred_element_type=f32)
        score = (score - square_sums(words)).reshape(tile // SUBLANES, SUBLANES, 2 * half)
        old = top[...]
        new = jnp.maximum(old, jnp.max(score, axis=0))
        total[...] = total[...] * jnp.exp(old - new) + jnp.sum(jnp.exp(score - new[None]), axis=0)
        top[...] = new

    best = jnp.max(top[...], axis=0, keepdims=True)
    lse[...] = best + jnp.log(jnp.sum(total[...] * jnp.exp(top[...] - best), axis=0, keepdims=True))


def stats_pass(core, first, second, words, early, tile):
    half, depth = first.shape
    count = words.shape[0]
    return pl.pallas_call(
        functools.partial(stats_kernel, tile),
        in_specs=[SMEM, ANY, ANY, VMEM, ANY],
        out_specs=VMEM,
        out_shape=jax.ShapeDtypeStruct((1, 2 * half), f32),
        scratch_shapes=[
            pltpu.VMEM((SUBLANES, 2 * half), f32),
            pltpu.VMEM((SUBLANES, 2 * half), f32),
            pltpu.VMEM((2 * half, depth), bf16),
            pltpu.SemaphoreType.DMA((2,)),
        ],
        name="stats_pass",
        cost_estimate=pl.CostEstimate(
            flops=4 * half * count * depth, bytes_accessed=2 * count * depth, transcendentals=0
        ),
        compiler_params=pltpu.CompilerParams(vmem_limit_bytes=24 * 2**20),
    )(core, first, second, words, early)


def row_fetches(core, pieces, block, sems, first):
    fetches = []
    for i, piece in enumerate(pieces):
        half = piece.shape[0]
        place = i - i % 2 + (core[0] if i % 2 == 0 else 1 - core[0])
        fetches.append(pltpu.make_async_copy(piece, block.at[span(place, half)], sems.at[first + i]))
    return fetches


def score_kernel(count, core, own, w_hbm, *refs):
    pieces, (logits, block, words, sems) = refs[:count], refs[count:]
    fetch = pltpu.make_async_copy(w_hbm.at[span(own[0], words.shape[0])], words, sems.at[count])
    fetch.start()
    fetches = row_fetches(core, pieces, block, sems, 0)
    for other in fetches:
        other.start()
    fetch.wait()
    sq = square_sums(words[...])
    for other in fetches:
        other.wait()
    score = lax.dot_general(words[...] * 2, block[...], NT, preferred_element_type=f32)
    logits[...] = score - sq


def score_pass(core, own, words, pieces, owned):
    depth = words.shape[1]
    rows = sum(piece.shape[0] for piece in pieces)
    return pl.pallas_call(
        functools.partial(score_kernel, len(pieces)),
        in_specs=[SMEM, SMEM, HBM] + [HBM] * len(pieces),
        out_specs=VMEM,
        scratch_shapes=[
            pltpu.VMEM((rows, depth), bf16),
            pltpu.VMEM((owned, depth), bf16),
            pltpu.SemaphoreType.DMA((len(pieces) + 1,)),
        ],
        out_shape=jax.ShapeDtypeStruct((owned, rows), f32),
        name="score_pass",
        cost_estimate=pl.CostEstimate(
            flops=2 * owned * rows * depth, bytes_accessed=2 * rows * depth, transcendentals=0
        ),
        compiler_params=pltpu.CompilerParams(vmem_limit_bytes=40 * 2**20),
    )(core, own, words, *pieces)


def last_kernel(count, tile, chunk, core, own, w_hbm, la_ref, lse_ref, *refs):
    near, direct = refs[:count], refs[count : 2 * count]
    out, block, words, assign, staged, sems, out_sems = refs[2 * count :]
    owned = words.shape[0]
    rows = la_ref.shape[1]
    fetch = pltpu.make_async_copy(w_hbm.at[span(own[0], owned)], words, sems.at[2 * count])
    fetch.start()
    fetches = row_fetches(core, near, block.at[pl.ds(rows, rows)], sems, 0)
    fetches += row_fetches(core, direct, block.at[pl.ds(0, rows)], sems, count)
    for other in fetches[:count]:
        other.start()
    assign[:, :rows] = jnp.exp(la_ref[...] - lse_ref[0:1]).astype(bf16)
    fetch.wait()
    for other in fetches[count:]:
        other.start()
    sq = square_sums(words[...])
    twice = words[...] * 2
    each = near[0].shape[0]
    for lo in range(0, rows, chunk):
        for other in fetches[lo // each : (lo + chunk) // each]:
            other.wait()
        at = slice(rows + lo, rows + lo + chunk)
        score = lax.dot_general(twice, block[at], NT, preferred_element_type=f32)
        assign[:, at] = jnp.exp(score - sq - lse_ref[1:2, lo : lo + chunk]).astype(bf16)
    for other in fetches[count:]:
        other.wait()
    sends = []
    for lo in range(0, owned, tile):
        at = slice(lo, lo + tile)
        sums = lax.dot_general(assign[at], block[...], NN, preferred_element_type=f32)
        counts = jnp.sum(assign[at].astype(f32), axis=1, keepdims=True)
        staged[at] = (sums + smoothing * words[at].astype(f32)) / (counts + smoothing)
        sends.append(pltpu.make_async_copy(staged.at[at], out.at[at], out_sems.at[lo // tile]))
        sends[-1].start()
    for send in sends:
        send.wait()


def last_pass(core, own, words, scored, lse, near, direct, owned, tile, chunk):
    depth = words.shape[1]
    rows = scored.shape[1]
    count = len(near)
    return pl.pallas_call(
        functools.partial(last_kernel, count, tile, chunk),
        in_specs=[SMEM, SMEM, HBM, VMEM, VMEM] + [HBM] * (2 * count),
        out_specs=HBM,
        scratch_shapes=[
            pltpu.VMEM((2 * rows, depth), bf16),
            pltpu.VMEM((owned, depth), bf16),
            pltpu.VMEM((owned, 2 * rows), bf16),
            pltpu.VMEM((owned, depth), f32),
            pltpu.SemaphoreType.DMA((2 * count + 1,)),
            pltpu.SemaphoreType.DMA((owned // tile,)),
        ],
        out_shape=jax.ShapeDtypeStruct((owned, depth), f32),
        name="last_pass",
        compiler_params=pltpu.CompilerParams(vmem_limit_bytes=50 * 2**20),
    )(core, own, words, scored, lse, *near, *direct)


def to_other(value, axis, flip):
    return lax.ppermute(value, axis, [(i, i ^ flip) for i in range(lax.axis_size(axis))])


def to_column(value, step):
    n = lax.axis_size("dp")
    table = []
    for book in range(2):
        for core in range(2):
            for d in range(n):
                here = (book * 2 + core) * n + d
                there = ((1 - book) * 2 + core) * n + (d ^ (2 * step))
                table.append((here, there))
    return lax.ppermute(value, ("pair", "code", "dp"), table)


def in_hbm(value):
    return pltpu.with_memory_space_constraint(value, pltpu.HBM)


def step(samples, codebooks):
    words = pltpu.with_memory_space_constraint(codebooks[0], pltpu.HBM)
    resident = pltpu.with_memory_space_constraint(codebooks[0], pltpu.VMEM)
    rows, _ = samples.shape
    n = lax.axis_size("dp")
    owned = words.shape[0] // n
    core = lax.axis_index("code").reshape(1)
    own = lax.axis_index("dp").reshape(1)
    mine, other = first_pass(
        core, pltpu.with_memory_space_constraint(samples, pltpu.HBM), words, 1024
    )
    theirs = to_other(other, "code", 1)
    residual = join(core, samples, mine, theirs)

    direct = [to_column(residual, i) for i in range(n // 2)]
    swapped = [to_other(direct[i], "code", 1) for i in range(n // 2)]
    near = [to_other(direct[i], "dp", 1) for i in range(n // 2)]
    near_swapped = [to_other(near[i], "code", 1) for i in range(n // 2)]

    early = early_pass(resident)
    lse = stats_pass(core, direct[0], swapped[0], resident, early, 1024)
    lse = jnp.logaddexp(lse, to_other(lse, "code", 1))
    flip = 1
    while flip < n:
        lse = jnp.concatenate([lse, to_other(lse, "dp", flip)], axis=0)
        flip *= 2
    lse = jnp.stack([lse[0::2].reshape(-1), lse[1::2].reshape(-1)])

    direct = [in_hbm(v) for pair in zip(direct, swapped) for v in pair]
    near = [in_hbm(v) for pair in zip(near, near_swapped) for v in pair]
    scored = score_pass(core, own, words, direct, owned)
    updated = last_pass(
        *(core, own, words, scored, lse, near, direct, owned, max(owned // 8, 128), 2 * rows),
    )
    return updated[None]


def solution(mesh):
    in_specs = (P("dp", None), P("pair", "code", None))
    out_specs = P("pair", ("code", "dp"), None)
    return jax.shard_map(step, mesh=mesh, in_specs=in_specs, out_specs=out_specs, check_vma=False)
```
